32 devices in a mesh: eig: 4 (over x, core), store: 8 (over z, y).
Axes of the slice: x: 2, y: 2, z: 4, core: 2. Of those that a mesh axis runs over, the one named last changes fastest.
Arguments:
- acts: bfloat16 [1024, 8192], P('store'), may hold values from -6 to 6
- basis: bfloat16 [8192, 8192], P('store', 'eig'), may hold values from -0.0625 to 0.0625
- eigvals: float32 [64, 8192], P(None, 'eig'), may hold values from 0.5 to 8
- projection: bfloat16 [8192, 64], P('eig'), may hold values from -0.0625 to 0.0625
- out_factor: float32 [1024, 64], P('store', 'eig'), may hold values from -6 to 6
- store: bfloat16 [16384, 4096], P('store', 'eig'), may hold values from -0.09375 to 0.09375
Outputs:
- scores: float32 [1024, 16384], P(None, ('store', 'eig'))
The draws below stay inside these ranges and needn't reach their ends.
All inputs are finite; a program needn't handle non-finite values.
Results may differ from the reference program's by a relative error of at most 0.0041.
Values may be sent and summed in bfloat16 or wider, within the bound.
No kernel may reach another device: no remote copies, remote signals or barrier semaphores. Data moves between devices by JAX's collectives and lax.ppermute only.
A program may use at most 128 MiB of HBM per device.

```python
import math
import jax
import jax.numpy as jnp
from jax import lax

D = 8192
K_OUT = 64
K_IN = 64
NQ = 1024
STORE = 16384
PROJ = 4096


def block_scale(own_key, extent, shards, smallest, largest):
    factor_of, own = 1.0, jax.random.fold_in(own_key, 6)
    for axis_at, shards_of in shards:
        heights = jnp.exp(jax.random.uniform(jax.random.fold_in(own, axis_at), (shards_of,), jnp.float32, smallest / len(shards), largest / len(shards)))
        factor_of = factor_of * jnp.repeat(heights, extent[axis_at] // shards_of).reshape([-1 if axis == axis_at else 1 for axis in range(len(extent))])
    return factor_of


def scatter_about(own_key, dims, spread, bound, pieces=(), held_as=jnp.bfloat16):
    drawn = jax.random.normal(own_key, dims, jnp.float32) * spread
    if len(pieces) > 0:
        drawn = block_scale(own_key, dims, pieces, -0.22, 0.18) * drawn
    return jnp.clip(drawn, min=-bound, max=bound).astype(held_as)


def setup_inputs(seed: int = 0) -> dict:
    seeds = jax.random.split(jax.random.key(seed), 7)
    acts = scatter_about(seeds[0], (NQ, D), 1.0, 6.0, ((0, 8),))
    basis = scatter_about(seeds[1], (D, D), D ** -0.5, 0.0625, ((0, 8), (1, 4)))
    eigvals = jnp.clip(jnp.exp(math.log(8.0) - 2.7725887 * jax.random.uniform(seeds[2], (K_OUT, D), jnp.float32) ** block_scale(seeds[2], (K_OUT, D), ((1, 4),), -0.2, 0.2)), 0.5, 8.0)
    projection = scatter_about(seeds[3], (D, K_IN), D ** -0.5, 0.0625, ((0, 4),))
    out_factor = scatter_about(seeds[4], (NQ, K_OUT), 1.0, 6.0, ((0, 8), (1, 4)), jnp.float32)
    store = scatter_about(seeds[5], (STORE, PROJ), PROJ ** -0.5, 0.09375, ((0, 8), (1, 4)))
    return dict(acts=acts, basis=basis, eigvals=eigvals, projection=projection, out_factor=out_factor, store=store)


damping = 0.1


def reference(acts, basis, eigvals, projection, out_factor, store):
    rotated = jnp.dot(acts, basis, preferred_element_type=jnp.float32)
    inverse = 1.0 / (eigvals + damping)

    def project_component(row_inverse):
        scaled = (rotated * row_inverse[None, :]).astype(jnp.bfloat16)
        return jnp.dot(scaled, projection, preferred_element_type=jnp.float32)

    summed = lax.map(project_component, inverse)
    summed = jnp.transpose(summed, (1, 0, 2))
    features = (summed * out_factor[:, :, None]).reshape(NQ, K_OUT * K_IN).astype(jnp.bfloat16)
    return jnp.dot(features, store.T, preferred_element_type=jnp.float32)
```

```python
import jax
import jax.numpy as jnp
from jax import lax
from jax.sharding import PartitionSpec as P

K_IN = 64


damping = 0.1


def hop_masks(n):
    bits = n.bit_length() - 1
    masks = [1] if bits % 2 else []
    for at in range(bits % 2, bits, 2):
        masks += [1 << at, 3 << at]
    return masks


def mask_of(masks, r):
    out = 0
    for k, m in enumerate(masks):
        if r >> k & 1:
            out ^= m
    return out


def split(total, parts, unit):
    units = total // unit
    sizes = [(units // parts + (p < units % parts)) * unit for p in range(parts)]
    return [size for size in sizes if size]


def make_body(n_eig, n_store):
    masks = hop_masks(n_store)
    levels = len(masks)

    def over_store(x, mask):
        return lax.ppermute(x, "store", [(s, s ^ mask) for s in range(n_store)])

    def over_eig(x, mask):
        return lax.ppermute(x, "eig", [(e, e ^ mask) for e in range(n_eig)])

    def nt(a, b):
        return lax.dot_general(a, b, (((1,), (1,)), ((), ())), preferred_element_type=jnp.float32)

    def body(acts, basis, eigvals, projection, out_factor, store):
        e = lax.axis_index("eig")
        s = lax.axis_index("store")
        core = e & 1
        queries, depth = acts.shape
        rows, columns = basis.shape
        half = queries // 2
        slab = store.shape[0] // n_eig
        kept = out_factor.shape[1]

        mine = lax.dynamic_slice(acts, (core * half, 0), (half, depth))
        blocks = []
        with jax.named_scope("spread"):
            for r in range(n_store):
                m = mask_of(masks, r)
                piece = lax.dynamic_slice(mine, (0, (s ^ m) * rows), (half, rows))
                blocks.append(piece if r == 0 else over_store(piece, m))

        top = jnp.stack([jnp.max(jnp.abs(acts)), jnp.max(jnp.abs(basis))]).astype(jnp.float32)
        top = jnp.broadcast_to(top[:, None, None], (2, 8, 128))
        with jax.named_scope("scale"):
            for m in masks:
                top = jnp.maximum(top, over_store(top, m))
        bound = jnp.maximum(top[0, 0, 0], 1e-15) * jnp.maximum(top[1, 0, 0], 1e-15)
        scale = 60000.0 / (depth * bound)
        unscale = depth * bound / 60000.0

        with jax.named_scope("spread_core"):
            other = over_eig(jnp.concatenate(blocks, axis=0), 1)
        other = [other[r * half : (r + 1) * half] for r in range(n_store)]

        def slab_at(rho):
            return lax.dynamic_slice(store, ((e ^ rho) * slab, 0), (slab, store.shape[1]))

        slabs_own = [slab_at(rho) for rho in range(0, n_eig, 2)]
        with jax.named_scope("store_core"):
            slabs_core = over_eig(jnp.concatenate([slab_at(rho) for rho in range(1, n_eig, 2)], axis=0), 1)
        slabs_core = [slabs_core[i * slab : (i + 1) * slab] for i in range(n_eig // 2)]

        inverse = 1.0 / (eigvals + damping)
        inverse = inverse.reshape(n_eig, kept, columns)
        inverse = jnp.concatenate([lax.dynamic_index_in_dim(inverse, e ^ rho, 0, keepdims=False) for rho in range(n_eig)])
        weights = inverse[:, None, :] * projection.T.astype(jnp.float32)[None, :, :]
        weights = weights.astype(jnp.bfloat16).reshape(n_eig * kept * K_IN, columns)

        widths = split(columns, levels, 128)

        def reduce_store(chunk):
            at, done = 0, []
            for g, width in enumerate(widths):
                part = basis[:, at : at + width]
                at += width
                order = [(g + k) % levels for k in range(levels)]
                held = list(range(n_store))
                total = None
                for k in order:
                    keep = [r for r in held if not r >> k & 1]
                    away = [r for r in held if r >> k & 1]
                    if total is None:
                        out = jnp.dot(jnp.concatenate([chunk[r] for r in away]), part, preferred_element_type=jnp.float32) * scale
                        out = out.astype(jnp.float16)
                        stay = jnp.dot(jnp.concatenate([chunk[r] for r in keep]), part, preferred_element_type=jnp.float32) * scale
                    else:
                        out = jnp.concatenate([total[held.index(r) * half : (held.index(r) + 1) * half] for r in away]).astype(jnp.float16)
                        stay = jnp.concatenate([total[held.index(r) * half : (held.index(r) + 1) * half] for r in keep])
                    with jax.named_scope("reduce"):
                        total = stay + over_store(out, masks[k]).astype(jnp.float32)
                    held = keep
                done.append(total)
            return jnp.concatenate(done, axis=1) * unscale

        def project(rotated):
            high = lax.reduce_precision(rotated, 8, 7)
            both = jnp.concatenate([high, rotated - high]).astype(jnp.bfloat16)
            out = nt(both, weights)
            return (out[:half] + out[half:]).reshape(half, n_eig, kept * K_IN)

        first = project(reduce_store(blocks))
        second = project(reduce_store(other))

        away = jnp.concatenate([second[:, 1::2], first[:, 1::2]])
        stay = jnp.concatenate([first[:, 0::2], second[:, 0::2]])
        with jax.named_scope("sum_core"):
            summed = stay + over_eig(away, 1)
        mask = 2
        while mask < n_eig:
            pairs = summed.reshape(queries, -1, 2, kept * K_IN)
            with jax.named_scope("sum_eig"):
                summed = pairs[:, :, 0] + over_eig(pairs[:, :, 1].astype(jnp.bfloat16), mask).astype(jnp.float32)
            mask *= 2
        summed = summed.reshape(queries, kept * K_IN)
        summed = jnp.where(core == 0, summed, jnp.concatenate([summed[half:], summed[:half]]))
        features = (summed.reshape(queries, kept, K_IN) * out_factor[:, :, None]).reshape(queries, kept * K_IN)
        features = features.astype(jnp.bfloat16)

        scores = jnp.zeros((queries * n_store, slab), jnp.float32)
        for r in range(0, n_store, 2):
            m = mask_of(masks, r)
            with jax.named_scope("gather"):
                here = features if r == 0 else over_store(features, m)
                there = over_store(here, masks[0])
            at = s ^ m
            low = (at & masks[0]) == 0
            pair = jnp.where(low, jnp.concatenate([here, there]), jnp.concatenate([there, here]))
            with jax.named_scope("gather_core"):
                pair_core = over_eig(pair, 1)
            parts = [nt(pair, a) + nt(pair_core, b) for a, b in zip(slabs_own, slabs_core)]
            mask = 2
            while mask < n_eig:
                sent = jnp.concatenate(parts[1::2], axis=1).astype(jnp.bfloat16)
                with jax.named_scope("scores_eig"):
                    got = over_eig(sent, mask).astype(jnp.float32)
                parts = [p + got[:, i * slab : (i + 1) * slab] for i, p in enumerate(parts[0::2])]
                mask *= 2
            scores = lax.dynamic_update_slice(scores, parts[0], ((at // 2) * 2 * queries, 0))
        return scores

    return body


def solution(mesh):
    placed = (
        P("store", None),
        P("store", "eig"),
        P(None, "eig"),
        P("eig", None),
        P("store", "eig"),
        P("store", "eig"),
    )
    body = make_body(mesh.shape["eig"], mesh.shape["store"])
    return jax.shard_map(body, mesh=mesh, in_specs=placed, out_specs=P(None, ("store", "eig")), check_vma=False)
```

```python
import jax
import jax.numpy as jnp
from jax import lax
from jax.sharding import PartitionSpec as P


K_IN = 64


damping = 0.1


SUMS = [(0, (0, 2), (0, 1, 2)), (0, (2, 4), (0, 1, 2)), (1, (0, 2), (1, 0, 2)), (1, (2, 4), (0, 1, 2))]
PLAN = [0, 2, 1, 0, 3, 1, 2, 0, 3, 1, 2, 3]


def hop_masks(n):
    bits = n.bit_length() - 1
    masks = [1] if bits % 2 else []
    for at in range(bits % 2, bits, 2):
        masks += [1 << at, 3 << at]
    return masks


def mask_of(masks, r):
    out = 0
    for k, m in enumerate(masks):
        if r >> k & 1:
            out ^= m
    return out


def make_body(n_eig, n_store):
    masks = hop_masks(n_store)
    levels = len(masks)

    def over_store(x, mask):
        return lax.ppermute(x, "store", [(s, s ^ mask) for s in range(n_store)])

    def over_eig(x, mask):
        return lax.ppermute(x, "eig", [(e, e ^ mask) for e in range(n_eig)])

    def nt(a, b):
        return lax.dot_general(a, b, (((1,), (1,)), ((), ())), preferred_element_type=jnp.float32)

    def body(acts, basis, eigvals, projection, out_factor, store):
        e = lax.axis_index("eig")
        s = lax.axis_index("store")
        core = e & 1
        queries, depth = acts.shape
        rows, columns = basis.shape
        half = queries // 2
        slab = store.shape[0] // n_eig
        kept = out_factor.shape[1]

        tallest = jnp.max(jnp.abs(acts)).astype(jnp.float32)
        shrink = jnp.exp2(-jnp.floor(jnp.log2(jnp.maximum(tallest, 1e-30))))

        mine = lax.dynamic_slice(acts, (core * half, 0), (half, depth))
        blocks = []
        for r in range(n_store):
            m = mask_of(masks, r)
            piece = lax.dynamic_slice(mine, (0, (s ^ m) * rows), (half, rows))
            piece = (piece.astype(jnp.float32) * shrink).astype(jnp.bfloat16)
            blocks.append(piece if r == 0 else over_store(piece, m))

        widest = jnp.broadcast_to(jnp.maximum(jnp.max(jnp.abs(basis)).astype(jnp.float32), 1e-30), (8, 128))
        near, group = {}, widest
        for k, m in enumerate(masks):
            got = over_store(jnp.stack([widest, group]), m)
            near[k] = got[0, 0, 0]
            group = jnp.maximum(group, got[1])
        unit = 2.0 / 60000.0
        own_bound = widest[0, 0] * rows * unit
        near_bound = {k: near[k] * rows * unit for k in near}
        group_bound = group[0, 0] * depth * unit

        own_other = lax.dynamic_slice(acts, ((1 - core) * half, s * rows), (half, rows))
        own_other = (own_other.astype(jnp.float32) * shrink).astype(jnp.bfloat16)
        other = [own_other] + [over_eig(block, 1) for block in blocks[1:]]

        class Sum:
            def __init__(self, name):
                self.half, (low, high), order = SUMS[name]
                self.part = basis[:, columns * low // 4 : columns * high // 4]
                self.chunk = (blocks, other)[self.half]
                self.order = order if levels == 3 else range(levels)
                self.held, self.total, self.at = list(range(n_store)), None, 0

            def open(self):
                k = self.order[self.at]
                keep = [r for r in self.held if not r >> k & 1]
                away = [r for r in self.held if r >> k & 1]
                if self.total is None:
                    out = jnp.dot(jnp.concatenate([self.chunk[r] for r in away]), self.part, preferred_element_type=jnp.float32)
                    self.stay = jnp.dot(jnp.concatenate([self.chunk[r] for r in keep]), self.part, preferred_element_type=jnp.float32)
                    out, self.unscale = out * (1.0 / own_bound), near_bound[k]
                else:
                    take = lambda r: self.total[self.held.index(r) * half : (self.held.index(r) + 1) * half]
                    out = jnp.concatenate([take(r) for r in away]) * (1.0 / group_bound)
                    self.stay, self.unscale = jnp.concatenate([take(r) for r in keep]), group_bound
                self.held = keep
                self.out = out.astype(jnp.float16)

            def send(self):
                self.got = over_store(self.out, masks[self.order[self.at]])
                self.at += 1

            def close(self):
                self.total = self.stay + self.got.astype(jnp.float32) * self.unscale

        sums = [Sum(name) for name in range(len(SUMS))]
        for one in sums:
            one.open()
        for one in sums:
            one.send()
        last = None
        for place, name in enumerate(PLAN if levels == 3 else list(range(len(SUMS))) * levels):
            one = sums[name]
            if last is not None and last is not one and last.at < levels:
                one.stay, last.out = lax.optimization_barrier((one.stay, last.out))
            if last is not None and last.at < levels:
                last.send()
            one.close()
            if one.at < levels:
                one.open()
            if place == 2:
                one.out, store = lax.optimization_barrier((one.out, store))
            if place == 3:
                one.out, eigvals = lax.optimization_barrier((one.out, eigvals))
            last = one

        def slab_at(rho):
            return lax.dynamic_slice(store, ((e ^ rho) * slab, 0), (slab, store.shape[1]))

        slabs = [slab_at(rho) for rho in range(0, n_eig, 2)]
        slabs_core = over_eig(jnp.concatenate([slab_at(rho) for rho in range(1, n_eig, 2)], axis=0), 1)
        slabs = [jnp.concatenate([a, slabs_core[i * slab : (i + 1) * slab]], axis=1) for i, a in enumerate(slabs)]
        slabs = lax.optimization_barrier(slabs)

        inverse = 1.0 / (eigvals + damping)
        inverse = inverse.reshape(n_eig, kept, columns)
        inverse = jnp.concatenate([lax.dynamic_index_in_dim(inverse, e ^ rho, 0, keepdims=False) for rho in range(n_eig)])
        weights = inverse[:, None, :] * projection.T.astype(jnp.float32)[None, :, :]
        weights = weights.astype(jnp.bfloat16).reshape(n_eig * kept * K_IN, columns)

        first, second = [
            jnp.concatenate([one.total for one in sums if one.half == h], axis=1) * (1.0 / shrink) for h in range(2)
        ]
        rotated = jnp.where(core == 0, jnp.concatenate([first, second]), jnp.concatenate([second, first]))
        high = lax.reduce_precision(rotated, 8, 7)
        both = jnp.concatenate([high, rotated - high]).astype(jnp.bfloat16)
        summed = nt(weights, both)
        summed = summed[:, :queries] + summed[:, queries:]

        mask = 1
        while mask < n_eig:
            pairs = summed.reshape(-1, 2, kept * K_IN, queries)
            away = pairs[:, 1].reshape(-1, queries)
            got = over_eig(away if mask == 1 else away.astype(jnp.bfloat16), mask)
            summed = pairs[:, 0].reshape(-1, queries) + got.astype(jnp.float32)
            mask *= 2
        features = (summed.T.reshape(queries, kept, K_IN) * out_factor[:, :, None]).reshape(queries, kept * K_IN)
        features = features.astype(jnp.bfloat16)

        scores = jnp.zeros((queries * n_store, slab), jnp.float32)
        for r in range(0, n_store, 2):
            m = mask_of(masks, r)
            here = features if r == 0 else over_store(features, m)
            there = over_store(here, masks[0])
            at = s ^ m
            pair = jnp.concatenate([here, there])
            pair_core = over_eig(pair, 1)
            parts = []
            width = store.shape[1]
            for both_cores in slabs:
                parts.append(nt(pair, both_cores[:, :width]) + nt(pair_core, both_cores[:, width:]))
            mask = 2
            while mask < n_eig:
                sent = jnp.concatenate(parts[1::2], axis=1).astype(jnp.bfloat16)
                got = over_eig(sent, mask).astype(jnp.float32)
                parts = [p + got[:, i * slab : (i + 1) * slab] for i, p in enumerate(parts[0::2])]
                mask *= 2
            scores = lax.dynamic_update_slice(scores, parts[0][:queries], (at * queries, 0))
            scores = lax.dynamic_update_slice(scores, parts[0][queries:], ((at ^ masks[0]) * queries, 0))
        return scores

    return body


def solution(mesh):
    placed = (
        P("store", None),
        P("store", "eig"),
        P(None, "eig"),
        P("eig", None),
        P("store", "eig"),
        P("store", "eig"),
    )
    body = make_body(mesh.shape["eig"], mesh.shape["store"])

    return jax.shard_map(body, mesh=mesh, in_specs=placed, out_specs=P(None, ("store", "eig")), check_vma=False)
```
